128 devices in a mesh: rows: 16 (over x, z), cols: 8 (over y, core).
Axes of the slice: x: 4, y: 4, z: 4, core: 2. Of those that a mesh axis runs over, the one named last changes fastest.
Arguments:
- panel_cols: bfloat16 [64, 32, 256, 128], P('rows', 'cols'), may hold values from -1.75 to 1.75
- pivot_inv: bfloat16 [32, 256, 256], P('cols'), may hold values from -0.375 to 0.375
- pivot_rows: bfloat16 [32, 48, 256, 128], P('rows', 'cols'), may hold values from -1.75 to 1.75
- target_factors: bfloat16 [64, 48, 256, 128], P('rows', 'cols'), may hold values from -5 to 5
- near_blocks: bfloat16 [64, 8, 256, 256], P('rows', 'cols'), may hold values from -6 to 6
- near_cols: int32 [64, 8], P('rows', 'cols'), may hold values from 0 to 5, as said below
- sketch: bfloat16 [48, 256, 64], P('cols'), may hold values from -6 to 6
Outputs:
- near_out: bfloat16 [64, 8, 256, 256], P('rows', 'cols')
- far_out: bfloat16 [64, 48, 256, 128], P('rows', 'cols')
The draws below stay inside these ranges and needn't reach their ends.
Inputs may be any that keep to these rules, and one draw needn't show every extreme that they name: `near_cols`: for every block row, the 1 entries of each group of slots s with equal s // 1 are distinct.
All inputs are finite; a program needn't handle non-finite values.
Results may differ from the reference program's by a relative error of at most 0.009.
Values may be sent and summed in bfloat16 or wider, within the bound.
A program may use at most 128 MiB of HBM per device.

```python
import math
import jax
import jax.numpy as jnp
from jax import lax

B = 256
R = 64
CB_DEV = 6
NNEAR_DEV = 1
KP = 32
NBR = 64
NBC = 48
NNEAR = 8
N_COLS = 8


def draw_near_cols(key, part):
    scores = jax.random.randint(key, (NBR, N_COLS, CB_DEV), 0, 65536)
    scores = scores * CB_DEV + jnp.arange(CB_DEV, dtype=jnp.int32)[None, None, :]
    order = jnp.argsort(scores, axis=-1)
    chosen = order[:, :, :NNEAR_DEV]
    return chosen.reshape(NBR, N_COLS * NNEAR_DEV).astype(jnp.int32)


def shard_levels(rng, extent, cuts, smallest, top_value):
    gain = 1.0
    for position, shards_of in cuts:
        steps = jax.random.uniform(jax.random.fold_in(jax.random.fold_in(rng, 6), position), (shards_of,), jnp.float32, smallest / len(cuts), top_value / len(cuts))
        gain = gain * jnp.repeat(jnp.exp(steps), extent[position] // shards_of).reshape((-1,) + (1,) * (len(extent) - 1 - position))
    return gain


def scatter_about(stream_key, dims, spread, reach, pieces=(), held_as=jnp.bfloat16):
    result = jax.random.normal(stream_key, dims, jnp.float32) * spread
    if len(pieces) > 0:
        result = shard_levels(stream_key, dims, pieces, -0.22, 0.18) * result
    return jnp.clip(result, min=-reach, max=reach).astype(held_as)


def setup_inputs(seed: int = 0) -> dict:
    seeds = jax.random.split(jax.random.key(seed), 8)
    return {
        "panel_cols": scatter_about(seeds[0], (NBR, KP, B, 2 * R), ((B * R * R * KP) ** -0.125), 1.75, ((0, 16), (1, 8))),
        "pivot_inv": scatter_about(seeds[1], (KP, B, B), B ** -0.5, 0.375, ((0, 8),)),
        "pivot_rows": scatter_about(seeds[2], (KP, NBC, B, 2 * R), ((B * R * R * KP) ** -0.125), 1.75, ((0, 16), (1, 8))),
        "target_factors": scatter_about(seeds[3], (NBR, NBC, B, 2 * R), 0.35, 5.0, ((0, 16), (1, 8))),
        "near_blocks": scatter_about(seeds[4], (NBR, NNEAR, B, B), 1.0, 6.0, ((0, 16), (1, 8))),
        "near_cols": draw_near_cols(jax.random.fold_in(seeds[7], 71), 0),
        "sketch": scatter_about(seeds[6], (NBC, B, R), 1.0, 6.0, ((0, 8),)),
    }


def product_of(form, left, right):
    return jnp.einsum(form, left.astype(jnp.float32), right.astype(jnp.float32), precision=lax.Precision.HIGHEST)

def row_update(left_row, rows_all, target_row, near_row, near_index, sketch):
    half = left_row.shape[-1] // 2
    root_size = math.sqrt(left_row.shape[1])
    left_x = left_row[..., :half]
    left_y = left_row[..., half:]
    pivot_p = rows_all[..., :half]
    pivot_q = rows_all[..., half:]
    mid_cores = product_of('kbr,kjbs->kjrs', left_y, pivot_p).astype(jnp.bfloat16)
    left_terms = product_of('kbr,kjrs->jkbs', left_x, mid_cores).astype(jnp.bfloat16)
    left_near = jnp.take(left_terms, near_index, axis=0)
    q_near = jnp.take(pivot_q, near_index, axis=1)
    update = product_of('nkbs,kncs->nbc', left_near, q_near)
    near_new = (near_row.astype(jnp.float32) - update).astype(jnp.bfloat16)
    column_ids = jnp.arange(target_row.shape[0], dtype=jnp.int32)
    is_near = jnp.any(near_index[:, None] == column_ids[None, :], axis=0)
    target_u = target_row[..., :half]
    target_v = target_row[..., half:]
    sketch_core = product_of('jbs,jbt->jst', target_v, sketch).astype(jnp.bfloat16)
    pivot_sketch = product_of('kjbs,jbt->jkst', pivot_q, sketch).astype(jnp.bfloat16)
    sampled = product_of('jbs,jst->jbt', target_u, sketch_core) - product_of('jkbs,jkst->jbt', left_terms, pivot_sketch)
    gram_matrix = jnp.einsum('jbs,jbt->jst', sampled, sampled, precision=lax.Precision.HIGHEST)
    factor_chol = jnp.linalg.cholesky(gram_matrix)
    orthonormal = lax.linalg.triangular_solve(factor_chol, sampled, left_side=False, lower=True, transpose_a=True)
    basis = (root_size * orthonormal).astype(jnp.bfloat16)
    basis_core = product_of('jbs,jbt->jst', target_u, basis).astype(jnp.bfloat16)
    left_core = product_of('jkbs,jbt->jkst', left_terms, basis).astype(jnp.bfloat16)
    weights_out = (product_of('jbs,jst->jbt', target_v, basis_core) - product_of('kjbs,jkst->jbt', pivot_q, left_core)) / root_size
    keep_far = jnp.where(is_near, 0.0, 1.0).astype(jnp.bfloat16)[:, None, None]
    far_new = jnp.concatenate([basis, weights_out.astype(jnp.bfloat16)], axis=-1) * keep_far
    return (near_new, far_new)

def reference(panel_cols, pivot_inv, pivot_rows, target_factors, near_blocks, near_cols, sketch):
    half = panel_cols.shape[-1] // 2
    col_left = panel_cols[..., :half]
    col_right = panel_cols[..., half:]
    pivot_right = product_of('kab,ikar->ikbr', pivot_inv, col_right).astype(jnp.bfloat16)
    panel_all = jnp.concatenate([col_left, pivot_right], axis=-1)
    slot_ids = jnp.arange(NNEAR, dtype=jnp.int32)
    offsets = slot_ids // NNEAR_DEV * CB_DEV
    global_cols = (near_cols + offsets[None, :]).astype(jnp.int32)

    def one_row(row_items):
        return row_update(row_items[0], pivot_rows, row_items[1], row_items[2], row_items[3], sketch)
    near_new, far_new = lax.map(one_row, (panel_all, target_factors, near_blocks, global_cols))
    return (near_new, far_new)
```

```python
import jax
import jax.numpy as jnp
from jax import lax
from jax.experimental import pallas as pl
from jax.experimental.pallas import tpu as pltpu
from jax.sharding import PartitionSpec as P

MESH = pl.DeviceIdType.MESH
BF = jnp.bfloat16
F32 = jnp.float32
HIGH = lax.Precision.HIGHEST
RING = 4


class Place:
    def __init__(self):
        self.row, self.col = lax.axis_index("rows"), lax.axis_index("cols")
        self.x, self.z = self.row // RING, self.row % RING
        self.y, self.core = self.col // 2, self.col % 2

    def at(self, axis, step):
        if axis == "x":
            return (lax.rem(self.x + step + RING, RING) * RING + self.z, self.col)
        if axis == "z":
            return (self.x * RING + lax.rem(self.z + step + RING, RING), self.col)
        if axis == "y":
            return (self.row, lax.rem(self.y + step + RING, RING) * 2 + self.core)
        return (self.row, self.y * 2 + (1 - self.core))


def row_slot(half, da, db):
    dx, dz = (da, db) if half == 0 else (db, da)
    return (dx % RING) * RING + dz % RING


def offsets(half, slot):
    return slot // RING, slot % RING


def dot_nt(left, right, **kw):
    return lax.dot_general(left, right, (((1,), (1,)), ((), ())), preferred_element_type=F32, **kw)


def dot_nn(left, right, **kw):
    return lax.dot_general(left, right, (((1,), (0,)), ((), ())), preferred_element_type=F32, **kw)


def kernel(
    near_col, own_p, own_q, own_panel, target, near, sketch_t, near_out, far_out,
    buf_p, buf_q, buf_panel, total, left, sampled, grams,
    send_sem, recv_sem, panel_send, panel_recv, local_sem,
):
    place = Place()
    locals_ = [
        pltpu.make_async_copy(own_p, buf_p.at[:, 0], local_sem.at[0]),
        pltpu.make_async_copy(own_q, buf_q.at[:, 0], local_sem.at[1]),
        pltpu.make_async_copy(own_panel, buf_panel.at[0], local_sem.at[2]),
    ]
    for c in locals_:
        c.start()
    barrier = pltpu.get_barrier_semaphore()
    for axis, step in (("x", 1), ("x", -1), ("z", 1), ("z", -1), ("y", 1), ("y", -1), ("c", 1)):
        pl.semaphore_signal(barrier, inc=1, device_id=place.at(axis, step), device_id_type=MESH)
    pl.semaphore_wait(barrier, 7)
    for c in locals_:
        c.wait()

    sends = []
    counts = [0, 0]
    bufs = (buf_p, buf_q)

    def row_send(half, da, db, ring, step, parts):
        axis = ("xz" if half == 0 else "zx")[ring]
        src = row_slot(half, da, db)
        dst = row_slot(half, da - step, db) if ring == 0 else row_slot(half, da, db - step)
        for part in parts:
            c = pltpu.make_async_remote_copy(
                src_ref=bufs[part].at[half, src], dst_ref=bufs[part].at[half, dst],
                send_sem=send_sem.at[counts[0]], recv_sem=recv_sem.at[half, dst, part],
                device_id=place.at(axis, step), device_id_type=MESH,
            )
            counts[0] += 1
            c.start()
            sends.append(c)

    def row_wait(half, da, db):
        dst = row_slot(half, da, db)
        for part in (0, 1):
            ref = bufs[part].at[half, dst]
            pltpu.make_async_copy(ref, ref, recv_sem.at[half, dst, part]).wait()

    def panel_slot(dy, dc):
        return (dy % RING) * 2 + dc

    def panel_send_to(dy, dc, axis, step, parts):
        src = panel_slot(dy, dc)
        dst = panel_slot(dy - step, dc) if axis == "y" else panel_slot(dy, 1 - dc)
        for part in parts:
            c = pltpu.make_async_remote_copy(
                src_ref=buf_panel.at[src, part], dst_ref=buf_panel.at[dst, part],
                send_sem=panel_send.at[counts[1]], recv_sem=panel_recv.at[dst, part],
                device_id=place.at(axis, step), device_id_type=MESH,
            )
            counts[1] += 1
            c.start()
            sends.append(c)

    def panel_wait(dy, dc):
        dst = panel_slot(dy, dc)
        for part in (0, 1):
            ref = buf_panel.at[dst, part]
            pltpu.make_async_copy(ref, ref, panel_recv.at[dst, part]).wait()

    both = (0, 1)

    def onward(step):
        return (0,) if step == 1 else (1,)

    def start_blocks():
        lane = lax.broadcasted_iota(jnp.int32, (256, 128), 1)

        def body(n, carry):
            uv = target[n]
            v_only = jnp.where(lane >= 64, uv, jnp.zeros_like(uv))
            u_high = pltpu.roll(uv.astype(F32), 64, 1).astype(BF)
            is_near = near_col[n // 6] == lax.rem(n, 6)
            total[n] = dot_nt(v_only, u_high) * jnp.where(is_near, 0.0, 1.0)
            return carry

        lax.fori_loop(0, 24, body, 0)

    def group(half, slots):
        zeros = jnp.zeros((64, 256), BF)
        for g, slot in enumerate(slots):
            dx, dz = offsets(half, slot)
            xs, zs = lax.rem(place.x + dx, RING), lax.rem(place.z + dz, RING)
            dy = lax.rem(xs - place.y + RING, RING)
            dc = lax.rem(zs // 2 + place.core, 2)
            at = dy * 2 + dc
            first = lax.rem(zs, 2) * 2
            for kk in (0, 1):
                yhat = buf_panel[at, 0, first + kk]
                mid = dot_nn(buf_p[half, slot, kk, 0], yhat[:128]) + dot_nn(buf_p[half, slot, kk, 1], yhat[128:])
                mid = mid.astype(BF)
                for i in range(4):
                    xt = buf_panel[at, 1, first + kk, 64 * i : 64 * i + 64, :]
                    xt = jnp.concatenate([xt, zeros] if i % 2 == 0 else [zeros, xt], axis=0)
                    pair = mid[:, 128 * (i // 2) : 128 * (i // 2) + 128]
                    term = dot_nn(pair, xt).astype(BF)
                    for j in range(3):
                        left[i * 3 + j, g * 128 + kk * 64 : g * 128 + kk * 64 + 64, :] = term[64 * j : 64 * j + 64]

        def body(n, carry):
            j = lax.rem(n, 3)
            i = n // 3
            q = jnp.concatenate([buf_q[half, s, j] for s in slots], axis=1)
            at = i * 6 + half * 3 + j
            total[at] = total[at] - dot_nn(q, left[n, : 128 * len(slots)])
            return carry

        lax.fori_loop(0, 12, body, 0)

    for half in both:
        for step in (1, -1):
            row_send(half, 0, 0, 0, step, both)
    for step in (1, -1):
        panel_send_to(0, 0, "y", step, both)
    panel_send_to(0, 0, "c", 1, both)
    for half in both:
        for step in (1, -1):
            row_send(half, 0, 0, 1, step, both)
    start_blocks()
    for half in both:
        for step in (1, -1):
            row_wait(half, -step, 0)
            row_send(half, -step, 0, 0, step, onward(step))
            for step2 in (1, -1):
                row_send(half, -step, 0, 1, step2, both)
    for step in (1, -1):
        panel_wait(-step, 0)
        panel_send_to(-step, 0, "y", step, onward(step))
        panel_send_to(-step, 0, "c", 1, both)
    for half in both:
        for step in (1, -1):
            row_wait(half, 0, -step)
            row_send(half, 0, -step, 1, step, onward(step))
    for half in both:
        row_wait(half, 2, 0)
        for step in (1, -1):
            row_send(half, 2, 0, 1, step, both)
    panel_wait(2, 0)
    panel_send_to(2, 0, "c", 1, both)
    for dy in (0, 1, -1, 2):
        panel_wait(dy, 1)
    for half in both:
        group(half, [row_slot(half, *d) for d in ((0, 0), (1, 0), (-1, 0), (0, 1))])
    for da in (1, -1):
        for half in both:
            for step in (1, -1):
                row_wait(half, da, -step)
                row_send(half, da, -step, 1, step, onward(step))
    for half in both:
        group(half, [row_slot(half, *d) for d in ((0, -1), (2, 0), (1, 1), (1, -1))])
    for half in both:
        for step in (1, -1):
            row_wait(half, 2, -step)
            row_send(half, 2, -step, 1, step, onward(step))
    for half in both:
        group(half, [row_slot(half, *d) for d in ((-1, 1), (-1, -1), (2, 1), (2, -1))])
    for half in both:
        for da in (0, 1, -1, 2):
            row_wait(half, da, 2)
        group(half, [row_slot(half, *d) for d in ((0, 2), (1, 2), (-1, 2), (2, 2))])

    lane2 = lax.broadcasted_iota(jnp.int32, (64, 128), 1)
    sub2 = lax.broadcasted_iota(jnp.int32, (64, 128), 0)
    eye = jnp.where(lane2 == sub2, 1.0, 0.0).astype(F32)

    def sample(n, carry):
        z = dot_nn(sketch_t[lax.rem(n, 6)], total[n].astype(BF))
        sampled[n] = z
        z2 = jnp.concatenate([z, z], axis=0)
        gram = dot_nt(z, z2, precision=HIGH)
        grams[pl.ds(n, 64, stride=24), :] = jnp.where(lane2 >= 64, gram, eye)
        return carry

    lax.fori_loop(0, 24, sample, 0)

    lane24 = lax.broadcasted_iota(jnp.int32, (24, 128), 1)

    def eliminate(low):
        def body(j, carry):
            at = pl.ds(pl.multiple_of(j * 24, 8), 24)
            row = grams[at, :]
            pivot = jnp.sum(jnp.where(lane24 == 64 + j, row, 0.0), axis=1, keepdims=True)
            row = row * lax.rsqrt(pivot)
            grams[at, :] = row
            after = jnp.where(lane24 > 64 + j, row, 0.0)
            for c in range(low + 1, 64):
                grams[24 * c : 24 * c + 24, :] = grams[24 * c : 24 * c + 24, :] - after[:, 64 + c : 65 + c] * row
            return carry

        lax.fori_loop(low, low + 16, body, 0)

    for low in (0, 16, 32, 48):
        eliminate(low)

    def finish(n, carry):
        inverse = grams[pl.ds(n, 64, stride=24), :][:, :64]
        basis_t = (16.0 * dot_nn(inverse, sampled[n], precision=HIGH)).astype(BF)
        weight_t = (dot_nt(basis_t, total[n].astype(BF)) * (1.0 / 16.0)).astype(BF)
        is_near = near_col[n // 6] == lax.rem(n, 6)
        both_t = jnp.concatenate([basis_t, weight_t], axis=0).astype(F32)
        out = both_t.T
        far_out[n] = jnp.where(is_near, jnp.zeros_like(out), out).astype(BF)
        return carry

    lax.fori_loop(0, 24, finish, 0)

    def finish_near(i, carry):
        acc = total[i * 6]
        for j in range(1, 6):
            acc = jnp.where(near_col[i] == j, total[i * 6 + j], acc)
        near_out[i] = (near[i].astype(F32) + acc.T).astype(BF)
        return carry

    lax.fori_loop(0, 4, finish_near, 0)
    for c in sends:
        c.wait_send()


def prepare_rows(pivot_rows):
    p = pivot_rows[..., :64].reshape(2, 2, 3, 2, 128, 64)
    p = p.transpose(1, 0, 3, 2, 5, 4).reshape(2, 2, 2, 192, 128)
    q = pivot_rows[..., 64:].reshape(2, 2, 3, 256, 64)
    q = q.transpose(1, 2, 3, 0, 4).reshape(2, 3, 256, 128)
    return p, q


def prepare_panel(panel_cols, pivot_inv):
    yhat = jnp.einsum("kab,ikar->kbir", pivot_inv, panel_cols[..., 64:], preferred_element_type=F32)
    yhat = yhat.astype(BF).reshape(4, 256, 256)
    x_t = panel_cols[..., :64].transpose(1, 0, 3, 2).reshape(4, 256, 256)
    return jnp.stack([yhat, x_t])


def per_device(panel_cols, pivot_inv, pivot_rows, target_factors, near_blocks, near_cols, sketch):
    own_p, own_q = prepare_rows(pivot_rows)
    own_panel = prepare_panel(panel_cols, pivot_inv)
    sketch_t = sketch.transpose(0, 2, 1)
    any_ = pl.BlockSpec(memory_space=pl.ANY)
    vmem = pl.BlockSpec(memory_space=pltpu.VMEM)
    smem = pl.BlockSpec(memory_space=pltpu.SMEM)
    dma = pltpu.SemaphoreType.DMA
    near_new, far_new = pl.pallas_call(
        kernel,
        name="gather_and_eliminate",
        out_shape=(
            jax.ShapeDtypeStruct((4, 256, 256), BF),
            jax.ShapeDtypeStruct((24, 256, 128), BF),
        ),
        in_specs=[smem, any_, any_, any_, vmem, vmem, vmem],
        out_specs=(vmem, vmem),
        scratch_shapes=[
            pltpu.VMEM((2, 16, 2, 2, 192, 128), BF),
            pltpu.VMEM((2, 16, 3, 256, 128), BF),
            pltpu.VMEM((8, 2, 4, 256, 256), BF),
            pltpu.VMEM((24, 256, 256), F32),
            pltpu.VMEM((12, 512, 256), BF),
            pltpu.VMEM((24, 64, 256), F32),
            pltpu.VMEM((64 * 24, 128), F32),
            dma((60,)),
            dma((2, 16, 2)),
            dma((16,)),
            dma((8, 2)),
            dma((3,)),
        ],
        compiler_params=pltpu.CompilerParams(
            collective_id=0, has_side_effects=True, vmem_limit_bytes=56 << 20
        ),
    )(
        near_cols.reshape(4), own_p, own_q, own_panel,
        target_factors.reshape(24, 256, 128), near_blocks.reshape(4, 256, 256), sketch_t,
    )
    return near_new.reshape(near_blocks.shape), far_new.reshape(target_factors.shape)


def solution(mesh):
    placed = (
        P("rows", "cols", None, None),
        P("cols", None, None),
        P("rows", "cols", None, None),
        P("rows", "cols", None, None),
        P("rows", "cols", None, None),
        P("rows", "cols"),
        P("cols", None, None),
    )
    return jax.shard_map(
        per_device,
        mesh=mesh,
        in_specs=placed,
        out_specs=(P("rows", "cols", None, None), P("rows", "cols", None, None)),
        check_vma=False,
    )
```

```python
import jax
import jax.numpy as jnp
from jax import lax
from jax.experimental import pallas as pl
from jax.experimental.pallas import tpu as pltpu
from jax.sharding import PartitionSpec as P

MESH = pl.DeviceIdType.MESH
BF = jnp.bfloat16
F32 = jnp.float32
HIGH = lax.Precision.HIGHEST
RING = 4
PANEL = 16


class Place:
    def __init__(self):
        self.row, self.col = lax.axis_index("rows"), lax.axis_index("cols")
        self.x, self.z = self.row // RING, self.row % RING
        self.y, self.core = self.col // 2, self.col % 2

    def at(self, axis, step):
        if axis == "x":
            return (lax.rem(self.x + step + RING, RING) * RING + self.z, self.col)
        if axis == "z":
            return (self.x * RING + lax.rem(self.z + step + RING, RING), self.col)
        if axis == "y":
            return (self.row, lax.rem(self.y + step + RING, RING) * 2 + self.core)
        return (self.row, self.y * 2 + (1 - self.core))


def row_slot(half, da, db):
    dx, dz = (da, db) if half == 0 else (db, da)
    return (dx % RING) * RING + dz % RING


def offsets(half, slot):
    return slot // RING, slot % RING


def dot_nt(left, right, **kw):
    return lax.dot_general(left, right, (((1,), (1,)), ((), ())), preferred_element_type=F32, **kw)


def dot_nn(left, right, **kw):
    return lax.dot_general(left, right, (((1,), (0,)), ((), ())), preferred_element_type=F32, **kw)


def kernel(
    near_col, rows_hbm, panel_hbm, inv_hbm, target_hbm, near_hbm, sketch_hbm, near_out, far_out,
    raw_rows, raw_panel, raw_inv, target, near, sketch_t, near_new, far_new,
    buf_p, buf_q, buf_panel, total, left, sampled, grams,
    send_sem, recv_sem, panel_send, panel_recv, local_sem, out_sem,
):
    place = Place()
    loads = [
        pltpu.make_async_copy(src, dst, local_sem.at[i])
        for i, (src, dst) in enumerate(
            (
                (rows_hbm, raw_rows), (panel_hbm, raw_panel), (inv_hbm, raw_inv),
                (target_hbm, target), (sketch_hbm, sketch_t), (near_hbm, near),
            )
        )
    ]
    for c in loads:
        c.start()
    barrier = pltpu.get_barrier_semaphore()
    for axis, step in (("x", 1), ("x", -1), ("z", 1), ("z", -1), ("y", 1), ("y", -1), ("c", 1)):
        pl.semaphore_signal(barrier, inc=1, device_id=place.at(axis, step), device_id_type=MESH)

    loads[0].wait()
    for j in range(6):
        half, jj = j // 3, j % 3
        for kk in (0, 1):
            buf_p[half, 0, kk, 64 * jj : 64 * jj + 64, :] = raw_rows[kk, j].T[:64]
        buf_q[half, 0, jj] = jnp.concatenate([raw_rows[0, j][:, 64:], raw_rows[1, j][:, 64:]], axis=1)
    pl.semaphore_wait(barrier, 7)

    sends = []
    counts = [0, 0]
    bufs = (buf_p, buf_q)

    def row_send(half, da, db, ring, step, part):
        axis = ("xz" if half == 0 else "zx")[ring]
        src = row_slot(half, da, db)
        dst = row_slot(half, da - step, db) if ring == 0 else row_slot(half, da, db - step)
        c = pltpu.make_async_remote_copy(
            src_ref=bufs[part].at[half, src], dst_ref=bufs[part].at[half, dst],
            send_sem=send_sem.at[counts[0]], recv_sem=recv_sem.at[half, dst, part],
            device_id=place.at(axis, step), device_id_type=MESH,
        )
        counts[0] += 1
        c.start()
        sends.append(c)

    def row_wait(half, da, db, part):
        dst = row_slot(half, da, db)
        ref = bufs[part].at[half, dst]
        pltpu.make_async_copy(ref, ref, recv_sem.at[half, dst, part]).wait()

    def panel_slot(dy, dc):
        return (dy % RING) * 2 + dc

    def panel_send_to(dy, dc, axis, step, part):
        src = panel_slot(dy, dc)
        dst = panel_slot(dy - step, dc) if axis == "y" else panel_slot(dy, 1 - dc)
        c = pltpu.make_async_remote_copy(
            src_ref=buf_panel.at[src, part], dst_ref=buf_panel.at[dst, part],
            send_sem=panel_send.at[counts[1]], recv_sem=panel_recv.at[dst, part],
            device_id=place.at(axis, step), device_id_type=MESH,
        )
        counts[1] += 1
        c.start()
        sends.append(c)

    def panel_wait(dy, dc, part):
        dst = panel_slot(dy, dc)
        ref = buf_panel.at[dst, part]
        pltpu.make_async_copy(ref, ref, panel_recv.at[dst, part]).wait()

    both = (0, 1)

    def onward(step):
        return 0 if step == 1 else 1

    def prepare_panel():
        for k in range(4):
            turned = [raw_panel[i, k].T for i in range(4)]
            for i in range(4):
                buf_panel[0, k, 1, 64 * i : 64 * i + 64, :] = turned[i][:64]
            y_t = jnp.concatenate([t[64:] for t in turned], axis=0)
            buf_panel[0, k, 0] = dot_nn(y_t, raw_inv[k]).astype(BF)

    def start_blocks():
        lane = lax.broadcasted_iota(jnp.int32, (256, 128), 1)

        def body(n, carry):
            uv = target[n]
            v_only = jnp.where(lane >= 64, uv, jnp.zeros_like(uv))
            u_high = pltpu.roll(uv.astype(F32), 64, 1).astype(BF)
            is_near = near_col[n // 6] == lax.rem(n, 6)
            total[n] = dot_nt(v_only, u_high) * jnp.where(is_near, 0.0, 1.0)
            return carry

        lax.fori_loop(0, 24, body, 0)

    def group(half, places):
        slots = [row_slot(half, *d) for d in places]
        zeros = jnp.zeros((64, 256), BF)
        todo = []
        for g, slot in enumerate(slots):
            dx, dz = offsets(half, slot)
            xs, zs = lax.rem(place.x + dx, RING), lax.rem(place.z + dz, RING)
            dy = lax.rem(xs - place.y + RING, RING)
            dc = lax.rem(zs // 2 + place.core, 2)
            at = dy * 2 + dc
            for kk in (0, 1):
                k = lax.rem(zs, 2) * 2 + kk
                mid = dot_nt(buf_p[half, slot, kk], buf_panel[at, k, 0]).astype(BF)
                todo.append((mid, at, k, g * 128 + kk * 64))
        for mid, at, k, low in todo:
            for i in range(4):
                xt = buf_panel[at, k, 1, 64 * i : 64 * i + 64, :]
                xt = jnp.concatenate([xt, zeros] if i % 2 == 0 else [zeros, xt], axis=0)
                pair = mid[:, 128 * (i // 2) : 128 * (i // 2) + 128]
                term = dot_nn(pair, xt).astype(BF)
                for j in range(3):
                    left[i * 3 + j, low : low + 64, :] = term[64 * j : 64 * j + 64]
        for j in range(3):
            q = jnp.concatenate([buf_q[half, s, j] for s in slots], axis=1)
            for i in range(4):
                at = i * 6 + half * 3 + j
                total[at] = total[at] - dot_nn(q, left[i * 3 + j, : 128 * len(slots)])

    for part in both:
        for half in both:
            for step in (1, -1):
                row_send(half, 0, 0, 0, step, part if step == 1 else 1 - part)
    loads[1].wait()
    loads[2].wait()
    prepare_panel()
    for k in range(4):
        for step in (1, -1):
            panel_send_to(0, 0, "y", step, k if step == 1 else (k + 2) % 4)
    for k in range(4):
        panel_send_to(0, 0, "c", 1, k)
    for part in both:
        for half in both:
            for step in (1, -1):
                row_send(half, 0, 0, 1, step, part if step == 1 else 1 - part)
    loads[3].wait()
    start_blocks()
    for first in (True, False):
        for half in both:
            for step in (1, -1):
                part = onward(step) if first else 1 - onward(step)
                row_wait(half, -step, 0, part)
                if first:
                    row_send(half, -step, 0, 0, step, part)
                for step2 in (1, -1):
                    row_send(half, -step, 0, 1, step2, part)
    for k in range(4):
        for step in (1, -1):
            part = k if step == 1 else (k + 2) % 4
            panel_wait(-step, 0, part)
            if k < 2:
                panel_send_to(-step, 0, "y", step, part)
            panel_send_to(-step, 0, "c", 1, part)

    def turn(half, da):
        for first in (True, False):
            for step in (1, -1):
                part = onward(step) if first else 1 - onward(step)
                row_wait(half, da, -step, part)
                if first:
                    row_send(half, da, -step, 1, step, part)

    for half in both:
        turn(half, 0)
    for half in both:
        for part in both:
            row_wait(half, 2, 0, part)
            for step in (1, -1):
                row_send(half, 2, 0, 1, step, part)
    for part in (0, 2, 1, 3):
        panel_wait(2, 0, part)
        panel_send_to(2, 0, "c", 1, part)
    for dy in (0, 1, -1, 2):
        for part in range(4):
            panel_wait(dy, 1, part)

    def last(half, das):
        for da in das:
            for part in both:
                row_wait(half, da, 2, part)

    group(0, ((0, 0), (1, 0), (-1, 0), (0, 1)))
    for half in both:
        turn(half, 1)
        turn(half, -1)
    group(1, ((0, 0), (1, 0), (-1, 0), (0, 1)))
    for half in both:
        turn(half, 2)
    for half in both:
        group(half, ((0, -1), (2, 0), (1, 1), (1, -1)))
    for half in both:
        group(half, ((-1, 1), (-1, -1), (2, 1), (2, -1)))
    for half in both:
        last(half, (0, 1))
        group(half, ((0, 2), (1, 2)))
    for half in both:
        last(half, (-1, 2))
        group(half, ((-1, 2), (2, 2)))

    for c in loads[4:]:
        c.wait()
    lane2 = lax.broadcasted_iota(jnp.int32, (64, 128), 1)
    sub2 = lax.broadcasted_iota(jnp.int32, (64, 128), 0)
    eye = jnp.where(lane2 == sub2, 1.0, 0.0).astype(F32)

    stores = []
    for i in range(4):
        acc = total[i * 6]
        for j in range(1, 6):
            acc = jnp.where(near_col[i] == j, total[i * 6 + j], acc)
        near_new[i] = (near[i].astype(F32) + acc.T).astype(BF)
    stores.append(pltpu.make_async_copy(near_new, near_out, out_sem.at[0]))
    stores[-1].start()

    for n in range(24):
        z = dot_nn(sketch_t[n % 6], total[n].astype(BF))
        sampled[n] = z
        z2 = jnp.concatenate([z, z], axis=0)
        gram = dot_nt(z, z2, precision=HIGH)
        grams[pl.ds(n, 64, stride=24), :] = jnp.where(lane2 >= 64, gram, eye)

    for base in range(0, 64, PANEL):
        rows = [grams[24 * c : 24 * c + 24, :] for c in range(base, base + PANEL)]
        for t in range(PANEL):
            row = rows[t]
            pivot = row[:, 64 + base + t : 65 + base + t]
            scaled = row * (1.0 / pivot)
            for u in range(t + 1, PANEL):
                rows[u] = rows[u] - row[:, 64 + base + u : 65 + base + u] * scaled
            rows[t] = row * lax.rsqrt(pivot)
            grams[24 * (base + t) : 24 * (base + t) + 24, :] = rows[t]
        after = base + PANEL
        if after < 64:
            for n in range(24):
                done = grams[pl.ds(24 * base + n, PANEL, stride=24), :]
                rest = pl.ds(24 * after + n, 64 - after, stride=24)
                grams[rest, :] = grams[rest, :] - dot_nn(done.T[64 + after :], done, precision=HIGH)

    for n in range(24):
        inverse = grams[pl.ds(n, 64, stride=24), :][:, :64]
        basis_t = (16.0 * dot_nn(inverse, sampled[n], precision=HIGH)).astype(BF)
        weight_t = (dot_nt(basis_t, total[n].astype(BF)) * (1.0 / 16.0)).astype(BF)
        out = jnp.concatenate([basis_t, weight_t], axis=0).T
        far_new[n] = jnp.where(near_col[n // 6] == n % 6, jnp.zeros_like(out), out)
        if n % 6 == 5:
            done = pl.ds(n - 5, 6)
            stores.append(pltpu.make_async_copy(far_new.at[done], far_out.at[done], out_sem.at[1 + n // 6]))
            stores[-1].start()

    for c in sends:
        c.wait_send()
    for c in stores:
        c.wait()


def per_device(panel_cols, pivot_inv, pivot_rows, target_factors, near_blocks, near_cols, sketch):
    any_ = pl.BlockSpec(memory_space=pl.ANY)
    smem = pl.BlockSpec(memory_space=pltpu.SMEM)
    dma = pltpu.SemaphoreType.DMA
    near_new, far_new = pl.pallas_call(
        kernel,
        name="gather_and_eliminate",
        out_shape=(
            jax.ShapeDtypeStruct((4, 256, 256), BF),
            jax.ShapeDtypeStruct((24, 256, 128), BF),
        ),
        in_specs=[smem] + [any_] * 6,
        out_specs=(any_, any_),
        scratch_shapes=[
            pltpu.VMEM((2, 6, 256, 128), BF),
            pltpu.VMEM((4, 4, 256, 128), BF),
            pltpu.VMEM((4, 256, 256), BF),
            pltpu.VMEM((24, 256, 128), BF),
            pltpu.VMEM((4, 256, 256), BF),
            pltpu.VMEM((6, 64, 256), BF),
            pltpu.VMEM((4, 256, 256), BF),
            pltpu.VMEM((24, 256, 128), BF),
            pltpu.VMEM((2, 16, 2, 192, 256), BF),
            pltpu.VMEM((2, 16, 3, 256, 128), BF),
            pltpu.VMEM((8, 4, 2, 256, 256), BF),
            pltpu.VMEM((24, 256, 256), F32),
            pltpu.VMEM((12, 512, 256), BF),
            pltpu.VMEM((24, 64, 256), F32),
            pltpu.VMEM((64 * 24, 128), F32),
            dma((60,)),
            dma((2, 16, 2)),
            dma((28,)),
            dma((8, 4)),
            dma((6,)),
            dma((5,)),
        ],
        compiler_params=pltpu.CompilerParams(
            collective_id=0, has_side_effects=True, vmem_limit_bytes=56 << 20
        ),
    )(
        near_cols.reshape(4), pivot_rows, panel_cols, pivot_inv,
        target_factors.reshape(24, 256, 128), near_blocks.reshape(4, 256, 256), sketch.transpose(0, 2, 1),
    )
    return near_new.reshape(near_blocks.shape), far_new.reshape(target_factors.shape)


def solution(mesh):
    placed = (
        P("rows", "cols", None, None),
        P("cols", None, None),
        P("rows", "cols", None, None),
        P("rows", "cols", None, None),
        P("rows", "cols", None, None),
        P("rows", "cols"),
        P("cols", None, None),
    )
    return jax.shard_map(
        per_device,
        mesh=mesh,
        in_specs=placed,
        out_specs=(P("rows", "cols", None, None), P("rows", "cols", None, None)),
        check_vma=False,
    )
```

```python
import jax
import jax.numpy as jnp
from jax import lax
from jax.experimental import pallas as pl
from jax.experimental.pallas import tpu as pltpu
from jax.sharding import PartitionSpec as P

MESH = pl.DeviceIdType.MESH
BF = jnp.bfloat16
F32 = jnp.float32
HIGH = lax.Precision.HIGHEST
RING = 4
PANEL = 16


def dot_split(left, right):
    left_high, right_high = left.astype(BF), right.astype(BF)
    left_low = (left - left_high.astype(F32)).astype(BF)
    right_low = (right - right_high.astype(F32)).astype(BF)
    return dot_nn(
        jnp.concatenate([left_high, left_low, left_high], axis=1),
        jnp.concatenate([right_high, right_high, right_low], axis=0),
    )


class Place:
    def __init__(self):
        self.row, self.col = lax.axis_index("rows"), lax.axis_index("cols")
        self.x, self.z = self.row // RING, self.row % RING
        self.y, self.core = self.col // 2, self.col % 2

    def at(self, axis, step):
        if axis == "x":
            return (lax.rem(self.x + step + RING, RING) * RING + self.z, self.col)
        if axis == "z":
            return (self.x * RING + lax.rem(self.z + step + RING, RING), self.col)
        if axis == "y":
            return (self.row, lax.rem(self.y + step + RING, RING) * 2 + self.core)
        return (self.row, self.y * 2 + (1 - self.core))


def row_slot(half, da, db):
    dx, dz = (da, db) if half == 0 else (db, da)
    return (dx % RING) * RING + dz % RING


def offsets(half, slot):
    return slot // RING, slot % RING


def dot_nt(left, right, **kw):
    return lax.dot_general(left, right, (((1,), (1,)), ((), ())), preferred_element_type=F32, **kw)


def dot_nn(left, right, **kw):
    return lax.dot_general(left, right, (((1,), (0,)), ((), ())), preferred_element_type=F32, **kw)


def kernel(
    near_col, rows_hbm, panel_hbm, inv_hbm, target_hbm, near_hbm, sketch_hbm, near_out, far_out,
    raw_rows, raw_panel, raw_inv, target, near, sketch_t, near_new, far_new,
    buf_p, buf_q, buf_panel, total, left, sampled, grams,
    send_sem, recv_sem, panel_send, panel_recv, local_sem, out_sem,
):
    place = Place()
    loads = [
        pltpu.make_async_copy(src, dst, local_sem.at[i])
        for i, (src, dst) in enumerate(
            (
                (rows_hbm, raw_rows), (panel_hbm, raw_panel), (inv_hbm, raw_inv),
                (target_hbm, target), (sketch_hbm, sketch_t), (near_hbm, near),
            )
        )
    ]
    for c in loads:
        c.start()
    barrier = pltpu.get_barrier_semaphore()
    for axis, step in (("x", 1), ("x", -1), ("z", 1), ("z", -1), ("y", 1), ("y", -1), ("c", 1)):
        pl.semaphore_signal(barrier, inc=1, device_id=place.at(axis, step), device_id_type=MESH)

    loads[0].wait()
    for j in range(6):
        half, jj = j // 3, j % 3
        for kk in (0, 1):
            buf_p[half, 0, kk, 64 * jj : 64 * jj + 64, :] = raw_rows[kk, j].T[:64]
        buf_q[half, 0, jj] = jnp.concatenate([raw_rows[0, j][:, 64:], raw_rows[1, j][:, 64:]], axis=1)
    pl.semaphore_wait(barrier, 7)

    sends = []
    counts = [0, 0]
    bufs = (buf_p, buf_q)

    def row_send(half, da, db, ring, step, part):
        axis = ("xz" if half == 0 else "zx")[ring]
        src = row_slot(half, da, db)
        dst = row_slot(half, da - step, db) if ring == 0 else row_slot(half, da, db - step)
        c = pltpu.make_async_remote_copy(
            src_ref=bufs[part].at[half, src], dst_ref=bufs[part].at[half, dst],
            send_sem=send_sem.at[counts[0]], recv_sem=recv_sem.at[half, dst, part],
            device_id=place.at(axis, step), device_id_type=MESH,
        )
        counts[0] += 1
        c.start()
        sends.append(c)

    def row_wait(half, da, db, part):
        dst = row_slot(half, da, db)
        ref = bufs[part].at[half, dst]
        pltpu.make_async_copy(ref, ref, recv_sem.at[half, dst, part]).wait()

    def panel_slot(dy, dc):
        return (dy % RING) * 2 + dc

    def panel_send_to(dy, dc, axis, step, part):
        src = panel_slot(dy, dc)
        dst = panel_slot(dy - step, dc) if axis == "y" else panel_slot(dy, 1 - dc)
        c = pltpu.make_async_remote_copy(
            src_ref=buf_panel.at[src, part], dst_ref=buf_panel.at[dst, part],
            send_sem=panel_send.at[counts[1]], recv_sem=panel_recv.at[dst, part],
            device_id=place.at(axis, step), device_id_type=MESH,
        )
        counts[1] += 1
        c.start()
        sends.append(c)

    def panel_wait(dy, dc, part):
        dst = panel_slot(dy, dc)
        ref = buf_panel.at[dst, part]
        pltpu.make_async_copy(ref, ref, panel_recv.at[dst, part]).wait()

    both = (0, 1)

    def onward(step):
        return 0 if step == 1 else 1

    def prepare_panel():
        for k in range(4):
            turned = [raw_panel[i, k].T for i in range(4)]
            for i in range(4):
                buf_panel[0, k, 1, 64 * i : 64 * i + 64, :] = turned[i][:64]
            y_t = jnp.concatenate([turned[i ^ (k % 2)][64:] for i in range(4)], axis=0)
            buf_panel[0, k, 0] = dot_nn(y_t, raw_inv[k]).astype(BF)

    def start_blocks():
        lane = lax.broadcasted_iota(jnp.int32, (256, 128), 1)

        def body(n, carry):
            uv = target[n]
            v_only = jnp.where(lane >= 64, uv, jnp.zeros_like(uv))
            u_high = pltpu.roll(uv.astype(F32), 64, 1).astype(BF)
            is_near = near_col[n // 6] == lax.rem(n, 6)
            total[n] = dot_nt(v_only, u_high) * jnp.where(is_near, 0.0, 1.0)
            return carry

        lax.fori_loop(0, 24, body, 0)

    def group(half, places):
        slots = [row_slot(half, *d) for d in places]
        low = lax.broadcasted_iota(jnp.int32, (192, 128), 1) < 64
        todo = []
        for slot in slots:
            dx, dz = offsets(half, slot)
            xs, zs = lax.rem(place.x + dx, RING), lax.rem(place.z + dz, RING)
            dy = lax.rem(xs - place.y + RING, RING)
            dc = lax.rem(zs // 2 + place.core, 2)
            at = dy * 2 + dc
            k = lax.rem(zs, 2) * 2
            mids = [dot_nt(buf_p[half, slot, kk], buf_panel[at, k + kk, 0]).astype(BF) for kk in (0, 1)]
            todo.append((mids, at, k))
        for g, (mids, at, k) in enumerate(todo):
            for q in (0, 1):
                one, two = (m[:, 128 * q : 128 * q + 128] for m in mids)
                none = jnp.zeros_like(one)
                for i in (2 * q, 2 * q + 1):
                    x_one, x_two = (buf_panel[at, k + kk, 1, 64 * i : 64 * i + 64, :] for kk in (0, 1))
                    if i % 2 == 0:
                        mid = jnp.concatenate([jnp.where(low, one, none), jnp.where(low, none, two)], axis=0)
                        x_t = jnp.concatenate([x_one, x_two], axis=0)
                    else:
                        mid = jnp.concatenate([jnp.where(low, none, one), jnp.where(low, two, none)], axis=0)
                        x_t = jnp.concatenate([x_two, x_one], axis=0)
                    term = dot_nn(mid, x_t).astype(BF)
                    for kk in (0, 1):
                        for j in range(3):
                            at_row = 192 * kk + 64 * j
                            left[i * 3 + j, g * 128 + kk * 64 : g * 128 + kk * 64 + 64, :] = term[at_row : at_row + 64]
        for j in range(3):
            q = jnp.concatenate([buf_q[half, s, j] for s in slots], axis=1)
            for i in range(4):
                at = i * 6 + half * 3 + j
                total[at] = total[at] - dot_nn(q, left[i * 3 + j, : 128 * len(slots)])

    for part in both:
        for half in both:
            for step in (1, -1):
                row_send(half, 0, 0, 0, step, part if step == 1 else 1 - part)
    loads[1].wait()
    loads[2].wait()
    prepare_panel()
    for k in range(4):
        for step in (1, -1):
            panel_send_to(0, 0, "y", step, k if step == 1 else (k + 2) % 4)
    for k in range(4):
        panel_send_to(0, 0, "c", 1, k)
    for part in both:
        for half in both:
            for step in (1, -1):
                row_send(half, 0, 0, 1, step, part if step == 1 else 1 - part)
    loads[3].wait()
    start_blocks()
    for first in (True, False):
        for half in both:
            for step in (1, -1):
                part = onward(step) if first else 1 - onward(step)
                row_wait(half, -step, 0, part)
                if first:
                    row_send(half, -step, 0, 0, step, part)
                for step2 in (1, -1):
                    row_send(half, -step, 0, 1, step2, part)
    for k in range(4):
        for step in (1, -1):
            part = k if step == 1 else (k + 2) % 4
            panel_wait(-step, 0, part)
            if k < 2:
                panel_send_to(-step, 0, "y", step, part)
            panel_send_to(-step, 0, "c", 1, part)

    def turn(half, da):
        for first in (True, False):
            for step in (1, -1):
                part = onward(step) if first else 1 - onward(step)
                row_wait(half, da, -step, part)
                if first:
                    row_send(half, da, -step, 1, step, part)

    for half in both:
        turn(half, 0)
    for half in both:
        for part in both:
            row_wait(half, 2, 0, part)
            for step in (1, -1):
                row_send(half, 2, 0, 1, step, part)
    for part in (0, 2, 1, 3):
        panel_wait(2, 0, part)
        panel_send_to(2, 0, "c", 1, part)
    for dy in (0, 1, -1, 2):
        for part in range(4):
            panel_wait(dy, 1, part)

    def last(half, das):
        for da in das:
            for part in both:
                row_wait(half, da, 2, part)

    group(0, ((0, 0), (1, 0), (-1, 0), (0, 1)))
    for half in both:
        turn(half, 1)
        turn(half, -1)
    group(1, ((0, 0), (1, 0), (-1, 0), (0, 1)))
    for half in both:
        turn(half, 2)
    for half in both:
        group(half, ((0, -1), (2, 0), (1, 1), (1, -1)))
    for half in both:
        group(half, ((-1, 1), (-1, -1), (2, 1), (2, -1)))
    for half in both:
        last(half, (0, 1, -1))
        group(half, ((0, 2), (1, 2), (-1, 2)))
    for half in both:
        last(half, (2,))
        group(half, ((2, 2),))

    for c in loads[4:]:
        c.wait()
    lane2 = lax.broadcasted_iota(jnp.int32, (64, 128), 1)
    sub2 = lax.broadcasted_iota(jnp.int32, (64, 128), 0)
    eye = jnp.where(lane2 == sub2, 1.0, 0.0).astype(F32)

    stores = []
    for i in range(4):
        acc = total[i * 6]
        for j in range(1, 6):
            acc = jnp.where(near_col[i] == j, total[i * 6 + j], acc)
        near_new[i] = (near[i].astype(F32) + acc.T).astype(BF)
    stores.append(pltpu.make_async_copy(near_new, near_out, out_sem.at[0]))
    stores[-1].start()

    for n in range(24):
        z = dot_nn(sketch_t[n % 6], total[n].astype(BF))
        sampled[n] = z
        z2 = jnp.concatenate([z, z], axis=0)
        gram = dot_nt(z, z2, precision=HIGH)
        grams[pl.ds(n, 64, stride=24), :] = jnp.where(lane2 >= 64, gram, eye)

    for base in range(0, 64, PANEL):
        rows = [grams[24 * c : 24 * c + 24, :] for c in range(base, base + PANEL)]
        for low in range(0, PANEL, 4):

            def entry(t, c):
                at = 64 + base + low + c
                return jnp.broadcast_to(rows[low + t][:, at : at + 1], (24, 128))

            corner = {(t, c): entry(t, c) for t in range(4) for c in range(t, 4)}
            for t in range(4):
                row = rows[low + t]
                inverse = 1.0 / corner[t, t]
                scaled = row * inverse
                for u in range(t + 1, 4):
                    rows[low + u] = rows[low + u] - corner[t, u] * scaled
                    factor = corner[t, u] * inverse
                    for c in range(u, 4):
                        corner[u, c] = corner[u, c] - factor * corner[t, c]
                for u in range(low + 4, PANEL):
                    rows[u] = rows[u] - row[:, 64 + base + u : 65 + base + u] * scaled
                rows[low + t] = row * lax.rsqrt(corner[t, t])
                at = 24 * (base + low + t)
                grams[at : at + 24, :] = rows[low + t]
        after = base + PANEL
        if after < 64:
            for n in range(24):
                done = grams[pl.ds(24 * base + n, PANEL, stride=24), :]
                rest = pl.ds(24 * after + n, 64 - after, stride=24)
                grams[rest, :] = grams[rest, :] - dot_nn(done.T[64 + after :], done, precision=HIGH)

    for n in range(24):
        inverse = grams[pl.ds(n, 64, stride=24), :][:, :64]
        basis_t = (16.0 * dot_split(inverse, sampled[n])).astype(BF)
        weight_t = (dot_nt(basis_t, total[n].astype(BF)) * (1.0 / 16.0)).astype(BF)
        out = jnp.concatenate([basis_t, weight_t], axis=0).T
        far_new[n] = jnp.where(near_col[n // 6] == n % 6, jnp.zeros_like(out), out)
        if n % 6 == 5:
            done = pl.ds(n - 5, 6)
            stores.append(pltpu.make_async_copy(far_new.at[done], far_out.at[done], out_sem.at[1 + n // 6]))
            stores[-1].start()

    for c in sends:
        c.wait_send()
    for c in stores:
        c.wait()


def hand_over(near_new, far_new, near_out, far_out, near, far, sem):
    whole = pl.ds(0, 4)
    pieces = [(near_new, near, near_out, whole)]
    pieces += [(far_new, far, far_out, pl.ds(4 * n, 4)) for n in range(6)]
    loads = [pltpu.make_async_copy(src.at[at], mid.at[at], sem.at[0, n]) for n, (src, mid, _, at) in enumerate(pieces)]
    stores = [pltpu.make_async_copy(mid.at[at], dst.at[at], sem.at[1, n]) for n, (_, mid, dst, at) in enumerate(pieces)]
    for c in loads:
        c.start()
    for load, store in zip(loads, stores):
        load.wait()
        store.start()
    for c in stores:
        c.wait()


def per_device(panel_cols, pivot_inv, pivot_rows, target_factors, near_blocks, near_cols, sketch):
    any_ = pl.BlockSpec(memory_space=pl.ANY)
    smem = pl.BlockSpec(memory_space=pltpu.SMEM)
    dma = pltpu.SemaphoreType.DMA
    near_new, far_new = pl.pallas_call(
        kernel,
        name="gather_and_eliminate",
        out_shape=(
            jax.ShapeDtypeStruct((4, 256, 256), BF),
            jax.ShapeDtypeStruct((24, 256, 128), BF),
        ),
        in_specs=[smem] + [any_] * 6,
        out_specs=(any_, any_),
        scratch_shapes=[
            pltpu.VMEM((2, 6, 256, 128), BF),
            pltpu.VMEM((4, 4, 256, 128), BF),
            pltpu.VMEM((4, 256, 256), BF),
            pltpu.VMEM((24, 256, 128), BF),
            pltpu.VMEM((4, 256, 256), BF),
            pltpu.VMEM((6, 64, 256), BF),
            pltpu.VMEM((4, 256, 256), BF),
            pltpu.VMEM((24, 256, 128), BF),
            pltpu.VMEM((2, 16, 2, 192, 256), BF),
            pltpu.VMEM((2, 16, 3, 256, 128), BF),
            pltpu.VMEM((8, 4, 2, 256, 256), BF),
            pltpu.VMEM((24, 256, 256), F32),
            pltpu.VMEM((12, 512, 256), BF),
            pltpu.VMEM((24, 64, 256), F32),
            pltpu.VMEM((64 * 24, 128), F32),
            dma((60,)),
            dma((2, 16, 2)),
            dma((28,)),
            dma((8, 4)),
            dma((6,)),
            dma((5,)),
        ],
        compiler_params=pltpu.CompilerParams(
            collective_id=0, has_side_effects=True, vmem_limit_bytes=56 << 20
        ),
    )(
        near_cols.reshape(4), pivot_rows, panel_cols, pivot_inv,
        target_factors.reshape(24, 256, 128), near_blocks.reshape(4, 256, 256), sketch.transpose(0, 2, 1),
    )
    near_new, far_new = pl.pallas_call(
        hand_over,
        name="hand_over",
        out_shape=(
            jax.ShapeDtypeStruct(near_new.shape, BF),
            jax.ShapeDtypeStruct(far_new.shape, BF),
        ),
        in_specs=[any_, any_],
        out_specs=(any_, any_),
        scratch_shapes=[pltpu.VMEM((4, 256, 256), BF), pltpu.VMEM((24, 256, 128), BF), dma((2, 7))],
    )(near_new, far_new)
    return near_new.reshape(near_blocks.shape), far_new.reshape(target_factors.shape)


def solution(mesh):
    placed = (
        P("rows", "cols", None, None),
        P("cols", None, None),
        P("rows", "cols", None, None),
        P("rows", "cols", None, None),
        P("rows", "cols", None, None),
        P("rows", "cols"),
        P("cols", None, None),
    )
    return jax.shard_map(
        per_device,
        mesh=mesh,
        in_specs=placed,
        out_specs=(P("rows", "cols", None, None), P("rows", "cols", None, None)),
        check_vma=False,
    )
```

```python
import jax
import jax.numpy as jnp
from jax import lax
from jax.experimental import pallas as pl
from jax.experimental.pallas import tpu as pltpu
from jax.sharding import PartitionSpec as P

MESH = pl.DeviceIdType.MESH
BF = jnp.bfloat16
F32 = jnp.float32
HIGH = lax.Precision.HIGHEST
RING = 4
PANEL = 16


def dot_split(left, right):
    left_high, right_high = left.astype(BF), right.astype(BF)
    left_low = (left - left_high.astype(F32)).astype(BF)
    right_low = (right - right_high.astype(F32)).astype(BF)
    return dot_nn(
        jnp.concatenate([left_high, left_low, left_high], axis=1),
        jnp.concatenate([right_high, right_high, right_low], axis=0),
    )


class Place:
    def __init__(self):
        self.row, self.col = lax.axis_index("rows"), lax.axis_index("cols")
        self.x, self.z = self.row // RING, self.row % RING
        self.y, self.core = self.col // 2, self.col % 2

    def at(self, axis, step):
        if axis == "x":
            return (lax.rem(self.x + step + RING, RING) * RING + self.z, self.col)
        if axis == "z":
            return (self.x * RING + lax.rem(self.z + step + RING, RING), self.col)
        if axis == "y":
            return (self.row, lax.rem(self.y + step + RING, RING) * 2 + self.core)
        return (self.row, self.y * 2 + (1 - self.core))


def row_slot(half, da, db):
    dx, dz = (da, db) if half == 0 else (db, da)
    return (dx % RING) * RING + dz % RING


def offsets(half, slot):
    return slot // RING, slot % RING


def dot_nt(left, right, **kw):
    return lax.dot_general(left, right, (((1,), (1,)), ((), ())), preferred_element_type=F32, **kw)


def dot_nn(left, right, **kw):
    return lax.dot_general(left, right, (((1,), (0,)), ((), ())), preferred_element_type=F32, **kw)


def kernel(
    near_col, rows_hbm, panel_hbm, inv_hbm, target_hbm, near_hbm, sketch_hbm, near_out, far_out,
    raw_rows, raw_panel, raw_inv, target, near, sketch_t, near_new, far_new,
    buf_p, buf_q, buf_panel, total, left, sampled, grams,
    send_sem, recv_sem, panel_send, panel_recv, local_sem, out_sem,
):
    place = Place()
    loads = [
        pltpu.make_async_copy(src, dst, local_sem.at[i])
        for i, (src, dst) in enumerate(
            (
                (rows_hbm, raw_rows), (panel_hbm, raw_panel), (inv_hbm, raw_inv),
                (target_hbm, target), (sketch_hbm, sketch_t), (near_hbm, near),
            )
        )
    ]
    loads[0].start()
    barrier = pltpu.get_barrier_semaphore()
    for axis, step in (("x", 1), ("x", -1), ("z", 1), ("z", -1), ("y", 1), ("y", -1), ("c", 1)):
        pl.semaphore_signal(barrier, inc=1, device_id=place.at(axis, step), device_id_type=MESH)

    loads[0].wait()
    for c in loads[1:]:
        c.start()
    for j in range(6):
        half, jj = j // 3, j % 3
        for kk in (0, 1):
            buf_p[half, 0, kk, 64 * jj : 64 * jj + 64, :] = raw_rows[kk, j].T[:64]
        buf_q[half, 0, jj] = jnp.concatenate([raw_rows[0, j][:, 64:], raw_rows[1, j][:, 64:]], axis=1)
    pl.semaphore_wait(barrier, 7)

    sends = []
    counts = [0, 0]
    bufs = (buf_p, buf_q)

    def row_send(half, da, db, ring, step, part):
        axis = ("xz" if half == 0 else "zx")[ring]
        src = row_slot(half, da, db)
        dst = row_slot(half, da - step, db) if ring == 0 else row_slot(half, da, db - step)
        c = pltpu.make_async_remote_copy(
            src_ref=bufs[part].at[half, src], dst_ref=bufs[part].at[half, dst],
            send_sem=send_sem.at[counts[0]], recv_sem=recv_sem.at[half, dst, part],
            device_id=place.at(axis, step), device_id_type=MESH,
        )
        counts[0] += 1
        c.start()
        sends.append(c)

    def row_wait(half, da, db, part):
        dst = row_slot(half, da, db)
        ref = bufs[part].at[half, dst]
        pltpu.make_async_copy(ref, ref, recv_sem.at[half, dst, part]).wait()

    def panel_slot(dy, dc):
        return (dy % RING) * 2 + dc

    def panel_send_to(dy, dc, axis, step, part):
        src = panel_slot(dy, dc)
        dst = panel_slot(dy - step, dc) if axis == "y" else panel_slot(dy, 1 - dc)
        c = pltpu.make_async_remote_copy(
            src_ref=buf_panel.at[src, part], dst_ref=buf_panel.at[dst, part],
            send_sem=panel_send.at[counts[1]], recv_sem=panel_recv.at[dst, part],
            device_id=place.at(axis, step), device_id_type=MESH,
        )
        counts[1] += 1
        c.start()
        sends.append(c)

    def panel_wait(dy, dc, part):
        dst = panel_slot(dy, dc)
        ref = buf_panel.at[dst, part]
        pltpu.make_async_copy(ref, ref, panel_recv.at[dst, part]).wait()

    both = (0, 1)

    def onward(step):
        return 0 if step == 1 else 1

    def prepare_panel():
        for k in range(4):
            turned = [raw_panel[i, k].T for i in range(4)]
            for i in range(4):
                buf_panel[0, k, 1, 64 * i : 64 * i + 64, :] = turned[i][:64]
            y_t = jnp.concatenate([turned[i ^ (k % 2)][64:] for i in range(4)], axis=0)
            buf_panel[0, k, 0] = dot_nn(y_t, raw_inv[k]).astype(BF)

    def start_blocks():
        lane = lax.broadcasted_iota(jnp.int32, (256, 128), 1)

        def body(n, carry):
            uv = target[n]
            v_only = jnp.where(lane >= 64, uv, jnp.zeros_like(uv))
            u_high = pltpu.roll(uv.astype(F32), 64, 1).astype(BF)
            is_near = near_col[n // 6] == lax.rem(n, 6)
            total[n] = dot_nt(v_only, u_high) * jnp.where(is_near, 0.0, 1.0)
            return carry

        lax.fori_loop(0, 24, body, 0)

    def group(half, places):
        slots = [row_slot(half, *d) for d in places]
        low = lax.broadcasted_iota(jnp.int32, (192, 128), 1) < 64
        todo = []
        for slot in slots:
            dx, dz = offsets(half, slot)
            xs, zs = lax.rem(place.x + dx, RING), lax.rem(place.z + dz, RING)
            dy = lax.rem(xs - place.y + RING, RING)
            dc = lax.rem(zs // 2 + place.core, 2)
            at = dy * 2 + dc
            k = lax.rem(zs, 2) * 2
            mids = [dot_nt(buf_p[half, slot, kk], buf_panel[at, k + kk, 0]).astype(BF) for kk in (0, 1)]
            todo.append((mids, at, k))
        for g, (mids, at, k) in enumerate(todo):
            for q in (0, 1):
                one, two = (m[:, 128 * q : 128 * q + 128] for m in mids)
                none = jnp.zeros_like(one)
                for i in (2 * q, 2 * q + 1):
                    x_one, x_two = (buf_panel[at, k + kk, 1, 64 * i : 64 * i + 64, :] for kk in (0, 1))
                    if i % 2 == 0:
                        mid = jnp.concatenate([jnp.where(low, one, none), jnp.where(low, none, two)], axis=0)
                        x_t = jnp.concatenate([x_one, x_two], axis=0)
                    else:
                        mid = jnp.concatenate([jnp.where(low, none, one), jnp.where(low, two, none)], axis=0)
                        x_t = jnp.concatenate([x_two, x_one], axis=0)
                    term = dot_nn(mid, x_t).astype(BF)
                    for kk in (0, 1):
                        for j in range(3):
                            at_row = 192 * kk + 64 * j
                            left[i * 3 + j, g * 128 + kk * 64 : g * 128 + kk * 64 + 64, :] = term[at_row : at_row + 64]
        for j in range(3):
            q = jnp.concatenate([buf_q[half, s, j] for s in slots], axis=1)
            for i in range(4):
                at = i * 6 + half * 3 + j
                total[at] = total[at] - dot_nn(q, left[i * 3 + j, : 128 * len(slots)])

    for part in both:
        for half in both:
            for step in (1, -1):
                row_send(half, 0, 0, 0, step, part if step == 1 else 1 - part)
    loads[1].wait()
    loads[2].wait()
    prepare_panel()
    for k in range(4):
        for step in (1, -1):
            panel_send_to(0, 0, "y", step, k if step == 1 else (k + 2) % 4)
    for k in range(4):
        panel_send_to(0, 0, "c", 1, k)
    for part in both:
        for half in both:
            for step in (1, -1):
                row_send(half, 0, 0, 1, step, part if step == 1 else 1 - part)
    loads[3].wait()
    start_blocks()
    for first in (True, False):
        for half in both:
            for step in (1, -1):
                part = onward(step) if first else 1 - onward(step)
                row_wait(half, -step, 0, part)
                if first:
                    row_send(half, -step, 0, 0, step, part)
                for step2 in (1, -1):
                    row_send(half, -step, 0, 1, step2, part)
    for k in range(4):
        for step in (1, -1):
            part = k if step == 1 else (k + 2) % 4
            panel_wait(-step, 0, part)
            if k < 2:
                panel_send_to(-step, 0, "y", step, part)
            panel_send_to(-step, 0, "c", 1, part)

    def turn(half, da):
        for first in (True, False):
            for step in (1, -1):
                part = onward(step) if first else 1 - onward(step)
                row_wait(half, da, -step, part)
                if first:
                    row_send(half, da, -step, 1, step, part)

    for half in both:
        turn(half, 0)
    for half in both:
        for part in both:
            row_wait(half, 2, 0, part)
            for step in (1, -1):
                row_send(half, 2, 0, 1, step, part)
    for part in (0, 2, 1, 3):
        panel_wait(2, 0, part)
        panel_send_to(2, 0, "c", 1, part)
    for dy in (0, 1, -1, 2):
        for part in range(4):
            panel_wait(dy, 1, part)

    def last(half, das):
        for da in das:
            for part in both:
                row_wait(half, da, 2, part)

    group(0, ((0, 0), (1, 0), (-1, 0), (0, 1)))
    for half in both:
        turn(half, 1)
        turn(half, -1)
    group(1, ((0, 0), (1, 0), (-1, 0), (0, 1)))
    for half in both:
        group(half, ((0, -1), (2, 0), (1, 1), (1, -1)))
    for half in both:
        turn(half, 2)
    for half in both:
        last(half, (0,))
        group(half, ((-1, 1), (-1, -1), (0, 2), (2, 1)))
    for half in both:
        last(half, (1, -1))
        group(half, ((2, -1), (1, 2), (-1, 2)))
    for half in both:
        last(half, (2,))
        group(half, ((2, 2),))

    for c in loads[4:]:
        c.wait()
    lane2 = lax.broadcasted_iota(jnp.int32, (64, 128), 1)
    sub2 = lax.broadcasted_iota(jnp.int32, (64, 128), 0)
    eye = jnp.where(lane2 == sub2, 1.0, 0.0).astype(F32)

    stores = []
    for i in range(4):
        acc = total[i * 6]
        for j in range(1, 6):
            acc = jnp.where(near_col[i] == j, total[i * 6 + j], acc)
        near_new[i] = (near[i].astype(F32) + acc.T).astype(BF)
    stores.append(pltpu.make_async_copy(near_new, near_out, out_sem.at[0]))
    stores[-1].start()

    for n in range(24):
        z = dot_nn(sketch_t[n % 6], total[n].astype(BF))
        sampled[n] = z
        high = z.astype(BF)
        rest = z - high.astype(F32)
        mid = rest.astype(BF)
        low = (rest - mid.astype(F32)).astype(BF)
        one = jnp.concatenate([high, mid, high, low, mid, high], axis=1)
        two = jnp.concatenate([high, high, mid, high, mid, low], axis=1)
        gram = dot_nt(one, jnp.concatenate([two, two], axis=0))
        grams[pl.ds(n, 64, stride=24), :] = jnp.where(lane2 >= 64, gram, eye)

    for base in range(0, 64, PANEL):
        rows = [grams[24 * c : 24 * c + 24, :] for c in range(base, base + PANEL)]
        for low in range(0, PANEL, 8):

            def entry(t, c):
                at = 64 + base + low + c
                return jnp.broadcast_to(rows[low + t][:, at : at + 1], (24, 128))

            corner = {(t, c): entry(t, c) for t in range(8) for c in range(t, 8)}
            for t in range(8):
                row = rows[low + t]
                inverse = 1.0 / corner[t, t]
                scaled = row * inverse
                for u in range(t + 1, 8):
                    rows[low + u] = rows[low + u] - corner[t, u] * scaled
                    factor = corner[t, u] * inverse
                    for c in range(u, 8):
                        corner[u, c] = corner[u, c] - factor * corner[t, c]
                for u in range(low + 8, PANEL):
                    rows[u] = rows[u] - row[:, 64 + base + u : 65 + base + u] * scaled
                rows[low + t] = row * lax.rsqrt(corner[t, t])
                at = 24 * (base + low + t)
                grams[at : at + 24, :] = rows[low + t]
        after = base + PANEL
        if after < 64:
            for n in range(24):
                done = grams[pl.ds(24 * base + n, PANEL, stride=24), :]
                rest = pl.ds(24 * after + n, 64 - after, stride=24)
                grams[rest, :] = grams[rest, :] - dot_nn(done.T[64 + after :], done, precision=HIGH)

    for n in range(24):
        inverse = grams[pl.ds(n, 64, stride=24), :][:, :64]
        basis_t = (16.0 * dot_split(inverse, sampled[n])).astype(BF)
        weight_t = (dot_nt(basis_t, total[n].astype(BF)) * (1.0 / 16.0)).astype(BF)
        out = jnp.concatenate([basis_t, weight_t], axis=0).T
        far_new[n] = jnp.where(near_col[n // 6] == n % 6, jnp.zeros_like(out), out)
        if n % 6 == 5:
            done = pl.ds(n - 5, 6)
            stores.append(pltpu.make_async_copy(far_new.at[done], far_out.at[done], out_sem.at[1 + n // 6]))
            stores[-1].start()

    for c in sends:
        c.wait_send()
    for c in stores:
        c.wait()


def hand_over(near_new, far_new, near_out, far_out, near, far, sem):
    whole = pl.ds(0, 4)
    pieces = [(near_new, near, near_out, whole)]
    pieces += [(far_new, far, far_out, pl.ds(4 * n, 4)) for n in range(6)]
    loads = [pltpu.make_async_copy(src.at[at], mid.at[at], sem.at[0, n]) for n, (src, mid, _, at) in enumerate(pieces)]
    stores = [pltpu.make_async_copy(mid.at[at], dst.at[at], sem.at[1, n]) for n, (_, mid, dst, at) in enumerate(pieces)]
    for c in loads:
        c.start()
    for load, store in zip(loads, stores):
        load.wait()
        store.start()
    for c in stores:
        c.wait()


def per_device(panel_cols, pivot_inv, pivot_rows, target_factors, near_blocks, near_cols, sketch):
    any_ = pl.BlockSpec(memory_space=pl.ANY)
    smem = pl.BlockSpec(memory_space=pltpu.SMEM)
    dma = pltpu.SemaphoreType.DMA
    near_new, far_new = pl.pallas_call(
        kernel,
        name="gather_and_eliminate",
        out_shape=(
            jax.ShapeDtypeStruct((4, 256, 256), BF),
            jax.ShapeDtypeStruct((24, 256, 128), BF),
        ),
        in_specs=[smem] + [any_] * 6,
        out_specs=(any_, any_),
        scratch_shapes=[
            pltpu.VMEM((2, 6, 256, 128), BF),
            pltpu.VMEM((4, 4, 256, 128), BF),
            pltpu.VMEM((4, 256, 256), BF),
            pltpu.VMEM((24, 256, 128), BF),
            pltpu.VMEM((4, 256, 256), BF),
            pltpu.VMEM((6, 64, 256), BF),
            pltpu.VMEM((4, 256, 256), BF),
            pltpu.VMEM((24, 256, 128), BF),
            pltpu.VMEM((2, 16, 2, 192, 256), BF),
            pltpu.VMEM((2, 16, 3, 256, 128), BF),
            pltpu.VMEM((8, 4, 2, 256, 256), BF),
            pltpu.VMEM((24, 256, 256), F32),
            pltpu.VMEM((12, 512, 256), BF),
            pltpu.VMEM((24, 64, 256), F32),
            pltpu.VMEM((64 * 24, 128), F32),
            dma((60,)),
            dma((2, 16, 2)),
            dma((28,)),
            dma((8, 4)),
            dma((6,)),
            dma((5,)),
        ],
        compiler_params=pltpu.CompilerParams(
            collective_id=0, has_side_effects=True, vmem_limit_bytes=56 << 20
        ),
    )(
        near_cols.reshape(4), pivot_rows, panel_cols, pivot_inv,
        target_factors.reshape(24, 256, 128), near_blocks.reshape(4, 256, 256), sketch.transpose(0, 2, 1),
    )
    near_new, far_new = pl.pallas_call(
        hand_over,
        name="hand_over",
        out_shape=(
            jax.ShapeDtypeStruct(near_new.shape, BF),
            jax.ShapeDtypeStruct(far_new.shape, BF),
        ),
        in_specs=[any_, any_],
        out_specs=(any_, any_),
        scratch_shapes=[pltpu.VMEM((4, 256, 256), BF), pltpu.VMEM((24, 256, 128), BF), dma((2, 7))],
    )(near_new, far_new)
    return near_new.reshape(near_blocks.shape), far_new.reshape(target_factors.shape)


def solution(mesh):
    placed = (
        P("rows", "cols", None, None),
        P("cols", None, None),
        P("rows", "cols", None, None),
        P("rows", "cols", None, None),
        P("rows", "cols", None, None),
        P("rows", "cols"),
        P("cols", None, None),
    )
    return jax.shard_map(
        per_device,
        mesh=mesh,
        in_specs=placed,
        out_specs=(P("rows", "cols", None, None), P("rows", "cols", None, None)),
        check_vma=False,
    )
```
